32 devices in a mesh: groups: 2 (over x), ctx: 16 (over z, y, core).
Axes of the slice: x: 2, y: 2, z: 4, core: 2. Of those that a mesh axis runs over, the one named last changes fastest.
Arguments:
- queries: bfloat16 [8192, 4096], P(('groups', 'ctx')), parts along dimension 0, may hold values from -160 to 160
- keys: bfloat16 [8192, 512], P(('groups', 'ctx')), parts along dimension 0, may hold values from -6 to 6
- values: bfloat16 [8192, 512], P(('groups', 'ctx')), parts along dimension 0, may hold values from -6 to 6
- doc_flags: int32 [64], P(('groups', 'ctx')), parts along dimension 0, may hold values from 0 to 1, as said below
Outputs:
- attention: bfloat16 [8192, 4096], P(('groups', 'ctx')), parts along dimension 0
The draws below stay inside these ranges and needn't reach their ends.
There are 2 independent parts, one for each index of `groups`. The reference program is written for one: setup_inputs(seed, part) draws one part's arguments, and reference() takes and returns one part's arrays. A program takes and returns all parts, laid end to end along the dimension named above; each array names one. Nothing has to cross between parts.
Inputs may be any that keep to these rules, and one draw needn't show every extreme that they name: `doc_flags`: block 0 starts a document; every document spans 1 to 6 blocks and one spans exactly 6 blocks.
All inputs are finite; a program needn't handle non-finite values.
Results may differ from the reference program's by a relative error of at most 0.0039.
Values may be sent and summed in bfloat16 or wider, within the bound.
A program may use at most 64 MiB of HBM per device.

```python
import jax
import jax.numpy as jnp
from jax import lax

HD = 128
KVH = 4
GROUP = 8
BLK = 128
ROUNDS = 4
TOK_DEV = 256
H = 32
TOKENS = 4096
NBLK = 32
MOST_BLK = 6
N_CTX = 16


def paired_draw(key):
    key_query, key_keys = jax.random.split(jax.random.fold_in(key, 7), 2)
    key_rows = jnp.clip(jax.random.normal(key_keys, (TOKENS, KVH * HD), jnp.float32), -6.0, 6.0)
    query_rows = jnp.clip(jax.random.normal(key_query, (TOKENS, H * HD), jnp.float32), -6.0, 6.0)
    return (query_rows, key_rows)


def draw_queries(key, part):
    return paired_draw(key)[0].astype(jnp.bfloat16)


def draw_keys(key, part):
    return paired_draw(key)[1].astype(jnp.bfloat16)


def draw_doc_flags(key, part):
    key_lengths, key_spot = jax.random.split(jax.random.fold_in(key, 11))
    lengths = jax.random.randint(key_lengths, (NBLK,), 1, MOST_BLK + 1)
    spot = jax.random.randint(key_spot, (), 0, NBLK // MOST_BLK)
    lengths = jnp.where(jnp.arange(NBLK) == spot, MOST_BLK, lengths).astype(jnp.int32)
    starts = jnp.cumsum(lengths).astype(jnp.int32) - lengths
    hits = jnp.arange(NBLK, dtype=jnp.int32)[:, None] == starts[None, :]
    return jnp.any(hits, axis=1).astype(jnp.int32)


def block_scale(key, extent, shards, low, largest):
    def one(dim, shards_of):
        steps = jax.random.uniform(jax.random.fold_in(jax.random.fold_in(key, 6), dim), (shards_of,), jnp.float32, low / len(shards), largest / len(shards))
        return jnp.repeat(jnp.exp(steps), extent[dim] // shards_of).reshape((-1,) + (1,) * (len(extent) - dim - 1))

    factor_of = one(*shards[0])
    for cut in shards[1:]:
        factor_of = factor_of * one(*cut)
    return factor_of


def normal_values(key, shape, scale, most, cuts=(), kind=jnp.bfloat16):
    drawn = scale * jax.random.normal(key, shape, jnp.float32)
    if cuts:
        drawn = drawn * block_scale(key, shape, cuts, -0.22, 0.18)
    return jnp.clip(drawn, -most, most).astype(kind)


def setup_inputs(seed: int = 0, part: int = 0) -> dict:
    seeds = jax.random.split(jax.random.key(seed), 5)
    part_splits = jax.random.split(jax.random.fold_in(seeds[4], part), 5)
    queries = draw_queries(jax.random.fold_in(jax.random.fold_in(seeds[4], part), 71), part)
    keys = draw_keys(jax.random.fold_in(jax.random.fold_in(seeds[4], part), 71), part)
    values = normal_values(part_splits[2], (TOKENS, KVH * HD), 1.0, 6.0, ((0, 16),))
    doc_flags = draw_doc_flags(jax.random.fold_in(jax.random.fold_in(seeds[4], part), 71), part)
    return {"queries": queries, "keys": keys, "values": values, "doc_flags": doc_flags}


NEG_FILL = -1.0e30


def reference(queries, keys, values, doc_flags):
    rows = TOK_DEV
    reach = ROUNDS * TOK_DEV
    lead = (ROUNDS - 1) * TOK_DEV
    scale = 1.0 / (HD ** 0.5)
    token_doc = jnp.repeat(jnp.cumsum(doc_flags).astype(jnp.int32), BLK, total_repeat_length=TOKENS)
    padded_doc = jnp.concatenate([jnp.full((lead,), -1, jnp.int32), token_doc])
    padded_keys = jnp.concatenate([jnp.zeros((lead, KVH * HD), keys.dtype), keys])
    padded_values = jnp.concatenate([jnp.zeros((lead, KVH * HD), values.dtype), values])

    def one_stretch(stretch):
        start = (stretch * rows).astype(jnp.int32)
        q_rows = lax.dynamic_slice_in_dim(queries, start, rows, 0)
        k_rows = lax.dynamic_slice_in_dim(padded_keys, start, reach, 0)
        v_rows = lax.dynamic_slice_in_dim(padded_values, start, reach, 0)
        doc_keys = lax.dynamic_slice_in_dim(padded_doc, start, reach, 0)
        doc_query = lax.dynamic_slice_in_dim(token_doc, start, rows, 0)
        query_pos = start + jnp.arange(rows, dtype=jnp.int32)
        key_pos = start - lead + jnp.arange(reach, dtype=jnp.int32)
        allowed = (key_pos[None, :] >= 0) & (key_pos[None, :] <= query_pos[:, None]) & (doc_keys[None, :] == doc_query[:, None])
        pieces = []
        for group in range(KVH):
            q_group = q_rows[:, group * GROUP * HD:(group + 1) * GROUP * HD].reshape(rows, GROUP, HD).astype(jnp.float32)
            k_group = k_rows[:, group * HD:(group + 1) * HD].astype(jnp.float32)
            v_group = v_rows[:, group * HD:(group + 1) * HD].astype(jnp.float32)
            scored = jnp.einsum('sjd,td->jst', q_group, k_group, precision=lax.Precision.HIGHEST) * scale
            scored = jnp.where(allowed[None], scored, NEG_FILL)
            top = jnp.max(scored, axis=2, keepdims=True)
            weights = jnp.exp(scored - top)
            total = jnp.sum(weights, axis=2)
            rounded = lax.optimization_barrier(weights.astype(jnp.bfloat16))
            mixed = jnp.einsum('jst,td->sjd', rounded.astype(jnp.float32), v_group, precision=lax.Precision.HIGHEST)
            pieces.append((mixed / total.T[:, :, None]).astype(jnp.bfloat16).reshape(rows, GROUP * HD))
        return jnp.concatenate(pieces, axis=1)

    stretches = lax.map(one_stretch, jnp.arange(N_CTX, dtype=jnp.int32))
    return stretches.reshape(TOKENS, H * HD)
```

```python
import functools
import math

import jax
import jax.numpy as jnp
from jax import lax
from jax.experimental import pallas as pl
from jax.experimental.pallas import tpu as pltpu
from jax.sharding import PartitionSpec as P

HD = 128
KVH = 4
GROUP = 8
BLK = 128
BACK = 5
NEG_FILL = -1e30
SCALE2 = math.log2(math.e) / math.sqrt(HD)
MESH = pl.DeviceIdType.MESH
HEADS_AT_ONCE = 2

ROWS = {3: (0, BLK), 2: (BLK, 2 * BLK), 1: (3 * BLK, 2 * BLK), 0: (5 * BLK, 2 * BLK)}
WINDOW = 7 * BLK
REACH = 6 * BLK


def kernel(
    n, q_hbm, k_hbm, v_hbm, flags_ref, o_hbm,
    q_buf, k_win, v_win, o_buf, bias, flags_out, flags_in,
    q_sem, own_sem, o_sem, send_sem, recv_sem, fwd_sem, fsend_sem, frecv_sem,
):
    me = lax.axis_index("ctx")
    core = lax.rem(me, 2)
    even, odd = core == 0, core == 1

    def window(win, g, back):
        start, size = ROWS[back]
        return win.at[g, pl.ds(start, size), :]

    def columns(g):
        return pl.ds(pl.multiple_of(g * HD, HD), HD)

    def q_copy(g):
        cols = pl.ds(pl.multiple_of(g * GROUP * HD, GROUP * HD), GROUP * HD)
        return pltpu.make_async_copy(q_hbm.at[:, cols], q_buf.at[g], q_sem.at[g])

    def o_copy(g):
        cols = pl.ds(pl.multiple_of(g * GROUP * HD, GROUP * HD), GROUP * HD)
        return pltpu.make_async_copy(o_buf.at[g], o_hbm.at[:, cols], o_sem.at[g])

    def own_copies(g):
        return [
            pltpu.make_async_copy(src.at[:, columns(g)], window(win, g, 0), own_sem.at[g, kv])
            for kv, (src, win) in enumerate(((k_hbm, k_win), (v_hbm, v_win)))
        ]

    def sends(g, back):
        size = ROWS[back][1]
        return [
            pltpu.make_async_remote_copy(
                src_ref=src.at[pl.ds(2 * BLK - size, size), columns(g)],
                dst_ref=window(win, g, back),
                send_sem=send_sem.at[g, back - 1, kv],
                recv_sem=recv_sem.at[g, back - 1, kv],
                device_id={"ctx": me + back},
                device_id_type=MESH,
            )
            for kv, (src, win) in enumerate(((k_hbm, k_win), (v_hbm, v_win)))
        ]

    def forwards(g, back):
        start, whole = ROWS[back]
        size = ROWS[back + 1][1]
        return [
            pltpu.make_async_remote_copy(
                src_ref=win.at[g, pl.ds(start + whole - size, size), :],
                dst_ref=window(win, g, back + 1),
                send_sem=fwd_sem.at[g, back - 1, kv],
                recv_sem=recv_sem.at[g, back, kv],
                device_id={"ctx": me + 1},
                device_id_type=MESH,
            )
            for kv, win in enumerate((k_win, v_win))
        ]

    def flag_send(back):
        return pltpu.make_async_remote_copy(
            src_ref=flags_out,
            dst_ref=flags_in.at[back - 1],
            send_sem=fsend_sem.at[back - 1],
            recv_sem=frecv_sem.at[back - 1],
            device_id={"ctx": me + back},
            device_id_type=MESH,
        )

    can_send = {
        1: me + 1 < n,
        2: even & (me + 2 < n),
        3: odd & (me + 3 < n),
    }
    direct = {1: me >= 1, 2: even & (me >= 2), 3: even & (me >= 3)}
    present = {back: me >= back for back in (1, 2, 3)}

    barrier = pltpu.get_barrier_semaphore()
    greet = [
        (1, me + 1 < n), (2, me + 2 < n), (3, can_send[3]),
        (-1, me >= 1), (-2, me >= 2), (-3, direct[3]),
    ]
    for step, there in greet:
        @pl.when(there)
        def _():
            pl.semaphore_signal(barrier, inc=1, device_id={"ctx": me + step}, device_id_type=MESH)

    for g in range(KVH):
        for copy in own_copies(g):
            copy.start()
        q_copy(g).start()
    flags_out[0:1, :] = jnp.full((1, BLK), flags_ref[0], jnp.int32)
    flags_out[1:2, :] = jnp.full((1, BLK), flags_ref[1], jnp.int32)
    flags_out[2:8, :] = jnp.zeros((6, BLK), jnp.int32)

    for back in (1, 2, 3):
        @pl.when(jnp.logical_not(present[back]))
        def _():
            start, size = ROWS[back]
            for win in (k_win, v_win):
                win[:, start:start + size, :] = jnp.zeros((KVH, size, HD), jnp.bfloat16)
            if back < 3:
                flags_in[back - 1] = jnp.zeros((8, BLK), jnp.int32)

    peers = jnp.int32(0)
    for _, there in greet:
        peers = peers + jnp.where(there, 1, 0)
    pl.semaphore_wait(barrier, peers)

    for back in (1, 2):
        @pl.when(me + back < n)
        def _():
            flag_send(back).start()
    for g in range(KVH):
        for back in (1, 2, 3):
            @pl.when(can_send[back])
            def _():
                for copy in sends(g, back):
                    copy.start()

    for back in (1, 2):
        @pl.when(present[back])
        def _():
            flag_send(back).wait_recv()

    mine = flags_out[...]
    begins = {0: mine[0:1], 1: mine[1:2]}
    for back in (1, 2):
        got = flags_in[back - 1]
        begins[-2 * back], begins[1 - 2 * back] = got[0:1], got[1:2]
    key_at = lax.broadcasted_iota(jnp.int32, (BLK, BLK), 0)
    row_at = lax.broadcasted_iota(jnp.int32, (BLK, BLK), 1)
    causal = jnp.where(key_at <= row_at, 0.0, NEG_FILL).astype(jnp.bfloat16)
    eye = (key_at == row_at).astype(jnp.bfloat16)
    for i in range(2):
        bias[i, BACK * BLK:(BACK + 1) * BLK, :] = causal
        hidden = jnp.zeros((1, BLK), jnp.float32)
        for b in range(i - 1, i - BACK - 1, -1):
            hidden = jnp.where(begins[b + 1] != 0, NEG_FILL, hidden)
            at = (b - i + BACK) * BLK
            bias[i, at:at + BLK, :] = jnp.broadcast_to(hidden, (BLK, BLK)).astype(jnp.bfloat16)
    ones = jnp.ones((REACH, HD), jnp.bfloat16)

    def one_group(g, carry):
        for back in (1, 2, 3):
            @pl.when(direct[back])
            def _():
                for copy in sends(g, back):
                    copy.wait_recv()
            if back < 3:
                @pl.when(even & present[back])
                def _():
                    for copy in forwards(g, back):
                        copy.start()
        for back in (2, 3):
            @pl.when(odd & present[back])
            def _():
                for copy in forwards(g, back - 1):
                    copy.wait_recv()
        for copy in own_copies(g):
            copy.wait()
        q_copy(g).wait()

        def some_heads(step, carry):
            for j in range(HEADS_AT_ONCE):
                cols = pl.ds(pl.multiple_of((step * HEADS_AT_ONCE + j) * HD, HD), HD)
                for i in range(2):
                    rows = pl.ds(i * BLK, BLK)
                    keys = pl.ds(i * BLK, REACH)
                    q = jnp.concatenate([q_buf[g, rows, cols], eye], axis=1)
                    k = jnp.concatenate([k_win[g, keys, :], bias[i]], axis=1)
                    s = lax.dot_general(
                        q, k, (((1,), (1,)), ((), ())), preferred_element_type=jnp.float32
                    )
                    top = jnp.max(s, axis=1, keepdims=True) * SCALE2
                    w = jnp.exp2(s * SCALE2 - top).astype(jnp.bfloat16)
                    v = jnp.concatenate([v_win[g, keys, :], ones], axis=1)
                    mixed = jnp.dot(w, v, preferred_element_type=jnp.float32)
                    o_buf[g, rows, cols] = (mixed[:, :HD] / mixed[:, HD:]).astype(jnp.bfloat16)
            return carry

        lax.fori_loop(0, GROUP // HEADS_AT_ONCE, some_heads, 0)
        o_copy(g).start()
        return carry

    lax.fori_loop(0, KVH, one_group, 0)

    for back in (1, 2):
        @pl.when(me + back < n)
        def _():
            flag_send(back).wait_send()
    for g in range(KVH):
        for back in (1, 2, 3):
            @pl.when(can_send[back])
            def _():
                for copy in sends(g, back):
                    copy.wait_send()
            if back < 3:
                @pl.when(even & present[back])
                def _():
                    for copy in forwards(g, back):
                        copy.wait_send()
        o_copy(g).wait()


def per_device(n, queries, keys, values, doc_flags):
    rows = queries.shape[0]
    dma = pltpu.SemaphoreType.DMA
    return pl.pallas_call(
        functools.partial(kernel, n),
        out_shape=jax.ShapeDtypeStruct(queries.shape, jnp.bfloat16),
        in_specs=[pl.BlockSpec(memory_space=pl.ANY)] * 3 + [pl.BlockSpec(memory_space=pltpu.SMEM)],
        out_specs=pl.BlockSpec(memory_space=pl.ANY),
        scratch_shapes=[
            pltpu.VMEM((KVH, rows, GROUP * HD), jnp.bfloat16),
            pltpu.VMEM((KVH, WINDOW, HD), jnp.bfloat16),
            pltpu.VMEM((KVH, WINDOW, HD), jnp.bfloat16),
            pltpu.VMEM((KVH, rows, GROUP * HD), jnp.bfloat16),
            pltpu.VMEM((2, REACH, BLK), jnp.bfloat16),
            pltpu.VMEM((8, BLK), jnp.int32),
            pltpu.VMEM((2, 8, BLK), jnp.int32),
            dma((KVH,)),
            dma((KVH, 2)),
            dma((KVH,)),
            dma((KVH, 3, 2)),
            dma((KVH, 3, 2)),
            dma((KVH, 2, 2)),
            dma((2,)),
            dma((2,)),
        ],
        compiler_params=pltpu.CompilerParams(
            collective_id=0, has_side_effects=True, vmem_limit_bytes=40 * 1024 * 1024
        ),
        name="window_attention",
    )(queries, keys, values, doc_flags)


def solution(mesh):
    spread = P(("groups", "ctx"), None)
    return jax.shard_map(
        functools.partial(per_device, mesh.shape["ctx"]),
        mesh=mesh,
        in_specs=(spread, spread, spread, P(("groups", "ctx"))),
        out_specs=spread,
        check_vma=False,
    )
```

```python
import functools
import math

import jax
import jax.numpy as jnp
from jax import lax
from jax.experimental import pallas as pl
from jax.experimental.pallas import tpu as pltpu
from jax.sharding import PartitionSpec as P

HD = 128
KVH = 4
GROUP = 8
BLK = 128
BACK = 5
NEG_FILL = -1e30
SCALE2 = math.log2(math.e) / math.sqrt(HD)
MESH = pl.DeviceIdType.MESH

ROWS = {3: (0, BLK), 2: (BLK, 2 * BLK), 1: (3 * BLK, 2 * BLK), 0: (5 * BLK, 2 * BLK)}
WINDOW = 7 * BLK
REACH = 6 * BLK


def kernel(
    n, q_hbm, k_hbm, v_hbm, flags_ref, o_hbm,
    q_buf, k_win, v_win, o_buf, bias, flags_out, flags_in,
    q_sem, own_sem, o_sem, send_sem, recv_sem, fwd_sem, fsend_sem, frecv_sem,
):
    me = lax.axis_index("ctx")
    core = lax.rem(me, 2)
    even, odd = core == 0, core == 1

    def window(win, g, back):
        start, size = ROWS[back]
        return win.at[g, pl.ds(start, size), :]

    def columns(g):
        return pl.ds(pl.multiple_of(g * HD, HD), HD)

    def q_copy(g):
        cols = pl.ds(pl.multiple_of(g * GROUP * HD, GROUP * HD), GROUP * HD)
        return pltpu.make_async_copy(q_hbm.at[:, cols], q_buf.at[g], q_sem.at[g])

    def o_copy(g):
        cols = pl.ds(pl.multiple_of(g * GROUP * HD, GROUP * HD), GROUP * HD)
        return pltpu.make_async_copy(o_buf.at[g], o_hbm.at[:, cols], o_sem.at[g])

    def own_copies(g):
        return [
            pltpu.make_async_copy(src.at[:, columns(g)], window(win, g, 0), own_sem.at[g, kv])
            for kv, (src, win) in enumerate(((k_hbm, k_win), (v_hbm, v_win)))
        ]

    def sends(g, back):
        size = ROWS[back][1]
        return [
            pltpu.make_async_remote_copy(
                src_ref=src.at[pl.ds(2 * BLK - size, size), columns(g)],
                dst_ref=window(win, g, back),
                send_sem=send_sem.at[g, back - 1, kv],
                recv_sem=recv_sem.at[g, back - 1, kv],
                device_id={"ctx": me + back},
                device_id_type=MESH,
            )
            for kv, (src, win) in enumerate(((k_hbm, k_win), (v_hbm, v_win)))
        ]

    def forwards(g, back):
        start, whole = ROWS[back]
        size = ROWS[back + 1][1]
        return [
            pltpu.make_async_remote_copy(
                src_ref=win.at[g, pl.ds(start + whole - size, size), :],
                dst_ref=window(win, g, back + 1),
                send_sem=fwd_sem.at[g, back - 1, kv],
                recv_sem=recv_sem.at[g, back, kv],
                device_id={"ctx": me + 1},
                device_id_type=MESH,
            )
            for kv, win in enumerate((k_win, v_win))
        ]

    def flag_send(back):
        return pltpu.make_async_remote_copy(
            src_ref=flags_out,
            dst_ref=flags_in.at[back - 1],
            send_sem=fsend_sem.at[back - 1],
            recv_sem=frecv_sem.at[back - 1],
            device_id={"ctx": me + back},
            device_id_type=MESH,
        )

    can_send = {
        1: me + 1 < n,
        2: even & (me + 2 < n),
        3: odd & (me + 3 < n),
    }
    direct = {1: me >= 1, 2: even & (me >= 2), 3: even & (me >= 3)}
    present = {back: me >= back for back in (1, 2, 3)}

    barrier = pltpu.get_barrier_semaphore()
    greet = [
        (1, me + 1 < n), (2, me + 2 < n), (3, can_send[3]),
        (-1, me >= 1), (-2, me >= 2), (-3, direct[3]),
    ]
    for step, there in greet:
        @pl.when(there)
        def _():
            pl.semaphore_signal(barrier, inc=1, device_id={"ctx": me + step}, device_id_type=MESH)

    for g in range(KVH):
        for copy in own_copies(g):
            copy.start()
        q_copy(g).start()
    flags_out[0:1, :] = jnp.full((1, BLK), flags_ref[0], jnp.int32)
    flags_out[1:2, :] = jnp.full((1, BLK), flags_ref[1], jnp.int32)
    flags_out[2:8, :] = jnp.zeros((6, BLK), jnp.int32)

    for back in (1, 2, 3):
        @pl.when(jnp.logical_not(present[back]))
        def _():
            start, size = ROWS[back]
            for win in (k_win, v_win):
                win[:, start:start + size, :] = jnp.zeros((KVH, size, HD), jnp.bfloat16)
            if back < 3:
                flags_in[back - 1] = jnp.zeros((8, BLK), jnp.int32)

    peers = jnp.int32(0)
    for _, there in greet:
        peers = peers + jnp.where(there, 1, 0)
    pl.semaphore_wait(barrier, peers)

    for back in (1, 2):
        @pl.when(me + back < n)
        def _():
            flag_send(back).start()
    for g in range(KVH):
        for back in (1, 2, 3):
            @pl.when(can_send[back])
            def _():
                for copy in sends(g, back):
                    copy.start()

    for back in (1, 2):
        @pl.when(present[back])
        def _():
            flag_send(back).wait_recv()

    mine = flags_out[...]
    begins = {0: mine[0:1], 1: mine[1:2]}
    for back in (1, 2):
        got = flags_in[back - 1]
        begins[-2 * back], begins[1 - 2 * back] = got[0:1], got[1:2]
    key_at = lax.broadcasted_iota(jnp.int32, (BLK, BLK), 0)
    row_at = lax.broadcasted_iota(jnp.int32, (BLK, BLK), 1)
    causal = jnp.where(key_at <= row_at, 0.0, NEG_FILL).astype(jnp.bfloat16)
    eye = (key_at == row_at).astype(jnp.bfloat16)
    for i in range(2):
        bias[i, BACK * BLK:(BACK + 1) * BLK, :] = causal
        hidden = jnp.zeros((1, BLK), jnp.float32)
        for b in range(i - 1, i - BACK - 1, -1):
            hidden = jnp.where(begins[b + 1] != 0, NEG_FILL, hidden)
            at = (b - i + BACK) * BLK
            bias[i, at:at + BLK, :] = jnp.broadcast_to(hidden, (BLK, BLK)).astype(jnp.bfloat16)
    ones = jnp.ones((REACH, HD), jnp.bfloat16)

    def one_group(g, carry):
        for back in (1, 2, 3):
            @pl.when(direct[back])
            def _():
                for copy in sends(g, back):
                    copy.wait_recv()
            if back < 3:
                @pl.when(even & present[back])
                def _():
                    for copy in forwards(g, back):
                        copy.start()
        for back in (2, 3):
            @pl.when(odd & present[back])
            def _():
                for copy in forwards(g, back - 1):
                    copy.wait_recv()
        for copy in own_copies(g):
            copy.wait()
        q_copy(g).wait()

        for i in range(2):
            rows = pl.ds(i * BLK, BLK)
            keys = pl.ds(i * BLK, REACH)
            heads = [pl.ds(j * HD, HD) for j in range(GROUP)]
            q = jnp.concatenate(
                [jnp.concatenate([q_buf[g, rows, head], eye], axis=1) for head in heads], axis=0
            )
            k = jnp.concatenate([k_win[g, keys, :], bias[i]], axis=1)
            s = lax.dot_general(
                q, k, (((1,), (1,)), ((), ())), preferred_element_type=jnp.float32
            )
            top = jnp.max(s, axis=1, keepdims=True) * SCALE2
            w = jnp.exp2(s * SCALE2 - top).astype(jnp.bfloat16)
            v = jnp.concatenate([v_win[g, keys, :], ones], axis=1)
            mixed = jnp.dot(w, v, preferred_element_type=jnp.float32)
            out = (mixed[:, :HD] / mixed[:, HD:]).astype(jnp.bfloat16)
            for j, head in enumerate(heads):
                o_buf[g, rows, head] = out[j * BLK:(j + 1) * BLK]

        o_copy(g).start()
        return carry

    lax.fori_loop(0, KVH, one_group, 0)

    for back in (1, 2):
        @pl.when(me + back < n)
        def _():
            flag_send(back).wait_send()
    for g in range(KVH):
        for back in (1, 2, 3):
            @pl.when(can_send[back])
            def _():
                for copy in sends(g, back):
                    copy.wait_send()
            if back < 3:
                @pl.when(even & present[back])
                def _():
                    for copy in forwards(g, back):
                        copy.wait_send()
        o_copy(g).wait()


def per_device(n, queries, keys, values, doc_flags):
    rows = queries.shape[0]
    dma = pltpu.SemaphoreType.DMA
    return pl.pallas_call(
        functools.partial(kernel, n),
        out_shape=jax.ShapeDtypeStruct(queries.shape, jnp.bfloat16),
        in_specs=[pl.BlockSpec(memory_space=pl.ANY)] * 3 + [pl.BlockSpec(memory_space=pltpu.SMEM)],
        out_specs=pl.BlockSpec(memory_space=pl.ANY),
        scratch_shapes=[
            pltpu.VMEM((KVH, rows, GROUP * HD), jnp.bfloat16),
            pltpu.VMEM((KVH, WINDOW, HD), jnp.bfloat16),
            pltpu.VMEM((KVH, WINDOW, HD), jnp.bfloat16),
            pltpu.VMEM((KVH, rows, GROUP * HD), jnp.bfloat16),
            pltpu.VMEM((2, REACH, BLK), jnp.bfloat16),
            pltpu.VMEM((8, BLK), jnp.int32),
            pltpu.VMEM((2, 8, BLK), jnp.int32),
            dma((KVH,)),
            dma((KVH, 2)),
            dma((KVH,)),
            dma((KVH, 3, 2)),
            dma((KVH, 3, 2)),
            dma((KVH, 2, 2)),
            dma((2,)),
            dma((2,)),
        ],
        compiler_params=pltpu.CompilerParams(
            collective_id=0, has_side_effects=True, vmem_limit_bytes=62 * 1024 * 1024
        ),
        name="window_attention",
    )(queries, keys, values, doc_flags)


def solution(mesh):
    spread = P(("groups", "ctx"), None)
    return jax.shard_map(
        functools.partial(per_device, mesh.shape["ctx"]),
        mesh=mesh,
        in_specs=(spread, spread, spread, P(("groups", "ctx"))),
        out_specs=spread,
        check_vma=False,
    )
```

```python
import functools
import math

import jax
import jax.numpy as jnp
from jax import lax
from jax.experimental import pallas as pl
from jax.experimental.pallas import tpu as pltpu
from jax.sharding import PartitionSpec as P

HD = 128
KVH = 4
GROUP = 8
BLK = 128
BACK = 5
NEG_FILL = -1e30
SCALE2 = math.log2(math.e) / math.sqrt(HD)
MESH = pl.DeviceIdType.MESH

ROWS = {3: (0, BLK), 2: (BLK, 2 * BLK), 1: (3 * BLK, 2 * BLK), 0: (5 * BLK, 2 * BLK)}
WINDOW = 7 * BLK
REACH = 6 * BLK


def attend(i, q_ref, k_ref, v_ref, bias, o_ref):
    rows, keys = pl.ds(i * BLK, BLK), pl.ds(i * BLK, REACH)
    heads = [pl.ds(j * HD, HD) for j in range(GROUP)]
    key_at = lax.broadcasted_iota(jnp.int32, (BLK, BLK), 0)
    row_at = lax.broadcasted_iota(jnp.int32, (BLK, BLK), 1)
    eye = (key_at == row_at).astype(jnp.bfloat16)
    q = jnp.concatenate(
        [jnp.concatenate([q_ref[rows, head], eye], axis=1) for head in heads], axis=0
    )
    k = jnp.concatenate([k_ref[keys, :], bias[i]], axis=1)
    s = lax.dot_general(q, k, (((1,), (1,)), ((), ())), preferred_element_type=jnp.float32)
    top = jnp.max(s, axis=1, keepdims=True) * SCALE2
    w = jnp.exp2(s * SCALE2 - top).astype(jnp.bfloat16)
    v = jnp.concatenate([v_ref[keys, :], jnp.ones((REACH, HD), jnp.bfloat16)], axis=1)
    mixed = jnp.dot(w, v, preferred_element_type=jnp.float32)
    out = (mixed[:, :HD] / mixed[:, HD:]).astype(jnp.bfloat16)
    for j, head in enumerate(heads):
        o_ref[rows, head] = out[j * BLK:(j + 1) * BLK]


def last_kernel(o_first, q_buf, k_win, v_win, bias, o_hbm, o_buf, sem):
    width, last = GROUP * HD, KVH - 1
    moves = []
    for g in range(last):
        move = pltpu.make_async_copy(
            o_first.at[g], o_hbm.at[:, pl.ds(g * width, width)], sem.at[g]
        )
        move.start()
        moves.append(move)
    for i in range(2):
        attend(i, q_buf.at[last], k_win.at[last], v_win.at[last], bias, o_buf)
        rows = pl.ds(i * BLK, BLK)
        move = pltpu.make_async_copy(
            o_buf.at[rows, :], o_hbm.at[rows, pl.ds(last * width, width)], sem.at[last + i]
        )
        move.start()
        moves.append(move)
    for move in moves:
        move.wait()


def kernel(
    n, q_hbm, k_hbm, v_hbm, flags_hbm,
    o_buf, q_buf, k_win, v_win, bias,
    flags_ref, flags_out, flags_in,
    q_sem, own_sem, flag_sem, send_sem, recv_sem, fwd_sem, fsend_sem, frecv_sem,
):
    me = lax.axis_index("ctx")
    core = lax.rem(me, 2)
    even, odd = core == 0, core == 1

    def window(win, g, back):
        start, size = ROWS[back]
        return win.at[g, pl.ds(start, size), :]

    def columns(g):
        return pl.ds(pl.multiple_of(g * HD, HD), HD)

    def q_copy(g):
        cols = pl.ds(pl.multiple_of(g * GROUP * HD, GROUP * HD), GROUP * HD)
        return pltpu.make_async_copy(q_hbm.at[:, cols], q_buf.at[g], q_sem.at[g])

    def own_copies(g):
        return [
            pltpu.make_async_copy(src.at[:, columns(g)], window(win, g, 0), own_sem.at[g, kv])
            for kv, (src, win) in enumerate(((k_hbm, k_win), (v_hbm, v_win)))
        ]

    def sends(g, back):
        size = ROWS[back][1]
        return [
            pltpu.make_async_remote_copy(
                src_ref=src.at[pl.ds(2 * BLK - size, size), columns(g)],
                dst_ref=window(win, g, back),
                send_sem=send_sem.at[g, back - 1, kv],
                recv_sem=recv_sem.at[g, back - 1, kv],
                device_id={"ctx": me + back},
                device_id_type=MESH,
            )
            for kv, (src, win) in enumerate(((k_hbm, k_win), (v_hbm, v_win)))
        ]

    def forwards(g, back):
        start, whole = ROWS[back]
        size = ROWS[back + 1][1]
        return [
            pltpu.make_async_remote_copy(
                src_ref=win.at[g, pl.ds(start + whole - size, size), :],
                dst_ref=window(win, g, back + 1),
                send_sem=fwd_sem.at[g, back - 1, kv],
                recv_sem=recv_sem.at[g, back, kv],
                device_id={"ctx": me + 1},
                device_id_type=MESH,
            )
            for kv, win in enumerate((k_win, v_win))
        ]

    def flag_send(back):
        return pltpu.make_async_remote_copy(
            src_ref=flags_out,
            dst_ref=flags_in.at[back - 1],
            send_sem=fsend_sem.at[back - 1],
            recv_sem=frecv_sem.at[back - 1],
            device_id={"ctx": me + back},
            device_id_type=MESH,
        )

    can_send = {
        1: me + 1 < n,
        2: even & (me + 2 < n),
        3: odd & (me + 3 < n),
    }
    direct = {1: me >= 1, 2: even & (me >= 2), 3: even & (me >= 3)}
    present = {back: me >= back for back in (1, 2, 3)}

    flag_copy = pltpu.make_async_copy(flags_hbm, flags_ref, flag_sem)
    flag_copy.start()
    barrier = pltpu.get_barrier_semaphore()
    greet = [
        (1, me + 1 < n), (2, me + 2 < n), (3, can_send[3]),
        (-1, me >= 1), (-2, me >= 2), (-3, direct[3]),
    ]
    for step, there in greet:
        @pl.when(there)
        def _():
            pl.semaphore_signal(barrier, inc=1, device_id={"ctx": me + step}, device_id_type=MESH)

    for g in range(KVH):
        for copy in own_copies(g):
            copy.start()
        q_copy(g).start()
    flag_copy.wait()
    flags_out[0:1, :] = jnp.full((1, BLK), flags_ref[0], jnp.int32)
    flags_out[1:2, :] = jnp.full((1, BLK), flags_ref[1], jnp.int32)
    flags_out[2:8, :] = jnp.zeros((6, BLK), jnp.int32)

    for back in (1, 2, 3):
        @pl.when(jnp.logical_not(present[back]))
        def _():
            start, size = ROWS[back]
            for win in (k_win, v_win):
                win[:, start:start + size, :] = jnp.zeros((KVH, size, HD), jnp.bfloat16)
            if back < 3:
                flags_in[back - 1] = jnp.zeros((8, BLK), jnp.int32)

    peers = jnp.int32(0)
    for _, there in greet:
        peers = peers + jnp.where(there, 1, 0)
    pl.semaphore_wait(barrier, peers)

    for back in (1, 2):
        @pl.when(me + back < n)
        def _():
            flag_send(back).start()
    for g in range(KVH):
        for back in (1, 2, 3):
            @pl.when(can_send[back])
            def _():
                for copy in sends(g, back):
                    copy.start()

    for back in (1, 2):
        @pl.when(present[back])
        def _():
            flag_send(back).wait_recv()

    mine = flags_out[...]
    begins = {0: mine[0:1], 1: mine[1:2]}
    for back in (1, 2):
        got = flags_in[back - 1]
        begins[-2 * back], begins[1 - 2 * back] = got[0:1], got[1:2]
    key_at = lax.broadcasted_iota(jnp.int32, (BLK, BLK), 0)
    row_at = lax.broadcasted_iota(jnp.int32, (BLK, BLK), 1)
    causal = jnp.where(key_at <= row_at, 0.0, NEG_FILL).astype(jnp.bfloat16)
    for i in range(2):
        bias[i, BACK * BLK:(BACK + 1) * BLK, :] = causal
        hidden = jnp.zeros((1, BLK), jnp.float32)
        for b in range(i - 1, i - BACK - 1, -1):
            hidden = jnp.where(begins[b + 1] != 0, NEG_FILL, hidden)
            at = (b - i + BACK) * BLK
            bias[i, at:at + BLK, :] = jnp.broadcast_to(hidden, (BLK, BLK)).astype(jnp.bfloat16)
    def arrive(g):
        for back in (1, 2, 3):
            @pl.when(direct[back])
            def _():
                for copy in sends(g, back):
                    copy.wait_recv()
            if back < 3:
                @pl.when(even & present[back])
                def _():
                    for copy in forwards(g, back):
                        copy.start()
        for back in (2, 3):
            @pl.when(odd & present[back])
            def _():
                for copy in forwards(g, back - 1):
                    copy.wait_recv()
        for copy in own_copies(g):
            copy.wait()
        q_copy(g).wait()

    def one_group(g, carry):
        arrive(g)
        for i in range(2):
            attend(i, q_buf.at[g], k_win.at[g], v_win.at[g], bias, o_buf.at[g])
        return carry

    lax.fori_loop(0, KVH - 1, one_group, 0)
    arrive(KVH - 1)

    for back in (1, 2):
        @pl.when(me + back < n)
        def _():
            flag_send(back).wait_send()
    for g in range(KVH):
        for back in (1, 2, 3):
            @pl.when(can_send[back])
            def _():
                for copy in sends(g, back):
                    copy.wait_send()
            if back < 3:
                @pl.when(even & present[back])
                def _():
                    for copy in forwards(g, back):
                        copy.wait_send()


def per_device(n, queries, keys, values, doc_flags):
    rows = queries.shape[0]
    dma = pltpu.SemaphoreType.DMA
    inputs = [
        pltpu.with_memory_space_constraint(x, pltpu.HBM)
        for x in (queries, keys, values, doc_flags)
    ]
    staged = pl.pallas_call(
        functools.partial(kernel, n),
        out_shape=[
            pltpu.VMEM((KVH - 1, rows, GROUP * HD), jnp.bfloat16),
            pltpu.VMEM((KVH, rows, GROUP * HD), jnp.bfloat16),
            pltpu.VMEM((KVH, WINDOW, HD), jnp.bfloat16),
            pltpu.VMEM((KVH, WINDOW, HD), jnp.bfloat16),
            pltpu.VMEM((2, REACH, BLK), jnp.bfloat16),
        ],
        in_specs=[pl.BlockSpec(memory_space=pltpu.HBM)] * 4,
        out_specs=[pl.BlockSpec(memory_space=pltpu.VMEM)] * 5,
        scratch_shapes=[
            pltpu.SMEM(doc_flags.shape, jnp.int32),
            pltpu.VMEM((8, BLK), jnp.int32),
            pltpu.VMEM((2, 8, BLK), jnp.int32),
            dma((KVH,)),
            dma((KVH, 2)),
            dma,
            dma((KVH, 3, 2)),
            dma((KVH, 3, 2)),
            dma((KVH, 2, 2)),
            dma((2,)),
            dma((2,)),
        ],
        compiler_params=pltpu.CompilerParams(
            collective_id=0, has_side_effects=True, vmem_limit_bytes=32 * 1024 * 1024
        ),
        name="window_attention",
    )(*inputs)
    return pl.pallas_call(
        last_kernel,
        out_shape=jax.ShapeDtypeStruct(queries.shape, jnp.bfloat16),
        in_specs=[pl.BlockSpec(memory_space=pltpu.VMEM)] * 5,
        out_specs=pl.BlockSpec(memory_space=pltpu.HBM),
        scratch_shapes=[pltpu.VMEM((rows, GROUP * HD), jnp.bfloat16), dma((KVH + 1,))],
        compiler_params=pltpu.CompilerParams(vmem_limit_bytes=32 * 1024 * 1024),
        name="last_group",
    )(*staged)


def solution(mesh):
    spread = P(("groups", "ctx"), None)
    return jax.shard_map(
        functools.partial(per_device, mesh.shape["ctx"]),
        mesh=mesh,
        in_specs=(spread, spread, spread, P(("groups", "ctx"))),
        out_specs=spread,
        check_vma=False,
    )
```

```python
import functools
import math

import jax
import jax.numpy as jnp
from jax import lax
from jax.experimental import pallas as pl
from jax.experimental.pallas import tpu as pltpu
from jax.sharding import PartitionSpec as P

HD = 128
KVH = 4
GROUP = 8
BLK = 128
BACK = 5
NEG_FILL = -1e30
SCALE2 = math.log2(math.e) / math.sqrt(HD)
MESH = pl.DeviceIdType.MESH
SEND_ORDER = (1, 2, 3)

ROWS = {3: (0, BLK), 2: (BLK, 2 * BLK), 1: (3 * BLK, 2 * BLK), 0: (5 * BLK, 2 * BLK)}
WINDOW = 7 * BLK
REACH = 6 * BLK


HEADS = [pl.ds(j * HD, HD) for j in range(GROUP)]


def weigh(i, q_ref, k_ref, bias):
    rows, keys = pl.ds(i * BLK, BLK), pl.ds(i * BLK, REACH)
    key_at = lax.broadcasted_iota(jnp.int32, (BLK, BLK), 0)
    row_at = lax.broadcasted_iota(jnp.int32, (BLK, BLK), 1)
    eye = (key_at == row_at).astype(jnp.bfloat16)
    q = jnp.concatenate(
        [jnp.concatenate([q_ref[rows, head], eye], axis=1) for head in HEADS], axis=0
    )
    k = jnp.concatenate([k_ref[keys, :], bias[i]], axis=1)
    s = lax.dot_general(q, k, (((1,), (1,)), ((), ())), preferred_element_type=jnp.float32)
    top = jnp.max(s, axis=1, keepdims=True) * SCALE2
    return jnp.exp2(s * SCALE2 - top).astype(jnp.bfloat16)


def mix(i, w, v_ref, o_ref):
    rows, keys = pl.ds(i * BLK, BLK), pl.ds(i * BLK, REACH)
    v = jnp.concatenate([v_ref[keys, :], jnp.ones((REACH, HD), jnp.bfloat16)], axis=1)
    mixed = jnp.dot(w, v, preferred_element_type=jnp.float32)
    out = (mixed[:, :HD] / mixed[:, HD:]).astype(jnp.bfloat16)
    for j, head in enumerate(HEADS):
        o_ref[rows, head] = out[j * BLK:(j + 1) * BLK]


def last_kernel(o_first, v_win, w_last, o_hbm, o_buf, sem):
    width, last = GROUP * HD, KVH - 1
    moves = []
    for g in range(last):
        move = pltpu.make_async_copy(
            o_first.at[g], o_hbm.at[:, pl.ds(g * width, width)], sem.at[g]
        )
        move.start()
        moves.append(move)
    for i in range(2):
        mix(i, w_last[i], v_win.at[last], o_buf)
        rows = pl.ds(i * BLK, BLK)
        move = pltpu.make_async_copy(
            o_buf.at[rows, :], o_hbm.at[rows, pl.ds(last * width, width)], sem.at[last + i]
        )
        move.start()
        moves.append(move)
    for move in moves:
        move.wait()


def kernel(
    n, q_hbm, k_hbm, v_hbm, flags_hbm,
    o_buf, v_win, w_last,
    q_buf, k_win, bias, flags_ref, flags_out, flags_in,
    q_sem, own_sem, flag_sem, send_sem, recv_sem, fwd_sem, fsend_sem, frecv_sem,
):
    me = lax.axis_index("ctx")
    core = lax.rem(me, 2)
    even, odd = core == 0, core == 1

    def window(win, g, back):
        start, size = ROWS[back]
        return win.at[g, pl.ds(start, size), :]

    def columns(g):
        return pl.ds(pl.multiple_of(g * HD, HD), HD)

    def q_copy(g):
        cols = pl.ds(pl.multiple_of(g * GROUP * HD, GROUP * HD), GROUP * HD)
        return pltpu.make_async_copy(q_hbm.at[:, cols], q_buf.at[g], q_sem.at[g])

    def own_copies(g):
        return [
            pltpu.make_async_copy(src.at[:, columns(g)], window(win, g, 0), own_sem.at[g, kv])
            for kv, (src, win) in enumerate(((k_hbm, k_win), (v_hbm, v_win)))
        ]

    def sends(g, back):
        size = ROWS[back][1]
        return [
            pltpu.make_async_remote_copy(
                src_ref=win.at[g, pl.ds(WINDOW - size, size), :],
                dst_ref=window(win, g, back),
                send_sem=send_sem.at[g, back - 1, kv],
                recv_sem=recv_sem.at[g, back - 1, kv],
                device_id={"ctx": me + back},
                device_id_type=MESH,
            )
            for kv, win in enumerate((k_win, v_win))
        ]

    def forwards(g, back):
        start, whole = ROWS[back]
        size = ROWS[back + 1][1]
        return [
            pltpu.make_async_remote_copy(
                src_ref=win.at[g, pl.ds(start + whole - size, size), :],
                dst_ref=window(win, g, back + 1),
                send_sem=fwd_sem.at[g, back - 1, kv],
                recv_sem=recv_sem.at[g, back, kv],
                device_id={"ctx": me + 1},
                device_id_type=MESH,
            )
            for kv, win in enumerate((k_win, v_win))
        ]

    def flag_send(back):
        return pltpu.make_async_remote_copy(
            src_ref=flags_out,
            dst_ref=flags_in.at[back - 1],
            send_sem=fsend_sem.at[back - 1],
            recv_sem=frecv_sem.at[back - 1],
            device_id={"ctx": me + back},
            device_id_type=MESH,
        )

    can_send = {
        1: me + 1 < n,
        2: even & (me + 2 < n),
        3: odd & (me + 3 < n),
    }
    direct = {1: me >= 1, 2: even & (me >= 2), 3: even & (me >= 3)}
    present = {back: me >= back for back in (1, 2, 3)}

    flag_copy = pltpu.make_async_copy(flags_hbm, flags_ref, flag_sem)
    flag_copy.start()
    barrier = pltpu.get_barrier_semaphore()
    greet = [
        (1, me + 1 < n), (2, me + 2 < n), (3, can_send[3]),
        (-1, me >= 1), (-2, me >= 2), (-3, direct[3]),
    ]
    for step, there in greet:
        @pl.when(there)
        def _():
            pl.semaphore_signal(barrier, inc=1, device_id={"ctx": me + step}, device_id_type=MESH)

    for g in range(KVH):
        for copy in own_copies(g):
            copy.start()
    for g in range(KVH):
        q_copy(g).start()
    flag_copy.wait()
    flags_out[0:1, :] = jnp.full((1, BLK), flags_ref[0], jnp.int32)
    flags_out[1:2, :] = jnp.full((1, BLK), flags_ref[1], jnp.int32)
    flags_out[2:8, :] = jnp.zeros((6, BLK), jnp.int32)

    for back in (1, 2, 3):
        @pl.when(jnp.logical_not(present[back]))
        def _():
            start, size = ROWS[back]
            for win in (k_win, v_win):
                win[:, start:start + size, :] = jnp.zeros((KVH, size, HD), jnp.bfloat16)
            if back < 3:
                flags_in[back - 1] = jnp.zeros((8, BLK), jnp.int32)

    peers = jnp.int32(0)
    for _, there in greet:
        peers = peers + jnp.where(there, 1, 0)
    pl.semaphore_wait(barrier, peers)

    for back in (1, 2):
        @pl.when(me + back < n)
        def _():
            flag_send(back).start()
    batches = [(g, (0, 1)) for g in range(KVH - 1)] + [(KVH - 1, (0,)), (KVH - 1, (1,))]
    for g, kinds in batches:
        for kv in kinds:
            own_copies(g)[kv].wait()
        for back in SEND_ORDER:
            @pl.when(can_send[back])
            def _():
                for kv in kinds:
                    sends(g, back)[kv].start()

    for back in (1, 2):
        @pl.when(present[back])
        def _():
            flag_send(back).wait_recv()

    mine = flags_out[...]
    begins = {0: mine[0:1], 1: mine[1:2]}
    for back in (1, 2):
        got = flags_in[back - 1]
        begins[-2 * back], begins[1 - 2 * back] = got[0:1], got[1:2]
    key_at = lax.broadcasted_iota(jnp.int32, (BLK, BLK), 0)
    row_at = lax.broadcasted_iota(jnp.int32, (BLK, BLK), 1)
    causal = jnp.where(key_at <= row_at, 0.0, NEG_FILL).astype(jnp.bfloat16)
    for i in range(2):
        bias[i, BACK * BLK:(BACK + 1) * BLK, :] = causal
        hidden = jnp.zeros((1, BLK), jnp.float32)
        for b in range(i - 1, i - BACK - 1, -1):
            hidden = jnp.where(begins[b + 1] != 0, NEG_FILL, hidden)
            at = (b - i + BACK) * BLK
            bias[i, at:at + BLK, :] = jnp.broadcast_to(hidden, (BLK, BLK)).astype(jnp.bfloat16)
    def arrive(g, kinds=(0, 1)):
        def pick(copies):
            return [copies[kv] for kv in kinds]

        for back in (1, 2, 3):
            @pl.when(direct[back])
            def _():
                for copy in pick(sends(g, back)):
                    copy.wait_recv()
            if back < 3:
                @pl.when(even & present[back])
                def _():
                    for copy in pick(forwards(g, back)):
                        copy.start()
        for back in (2, 3):
            @pl.when(odd & present[back])
            def _():
                for copy in pick(forwards(g, back - 1)):
                    copy.wait_recv()
        if 0 in kinds:
            q_copy(g).wait()

    def one_group(g, carry):
        arrive(g)
        for i in range(2):
            mix(i, weigh(i, q_buf.at[g], k_win.at[g], bias), v_win.at[g], o_buf.at[g])
        return carry

    lax.fori_loop(0, KVH - 1, one_group, 0)
    arrive(KVH - 1, (0,))
    for i in range(2):
        w_last[i] = weigh(i, q_buf.at[KVH - 1], k_win.at[KVH - 1], bias)
    arrive(KVH - 1, (1,))

    for back in (1, 2):
        @pl.when(me + back < n)
        def _():
            flag_send(back).wait_send()
    for g in range(KVH):
        for back in (1, 2, 3):
            @pl.when(can_send[back])
            def _():
                for copy in sends(g, back):
                    copy.wait_send()
            if back < 3:
                @pl.when(even & present[back])
                def _():
                    for copy in forwards(g, back):
                        copy.wait_send()


def per_device(n, queries, keys, values, doc_flags):
    rows = queries.shape[0]
    dma = pltpu.SemaphoreType.DMA
    inputs = [
        pltpu.with_memory_space_constraint(x, pltpu.HBM)
        for x in (queries, keys, values, doc_flags)
    ]
    staged = pl.pallas_call(
        functools.partial(kernel, n),
        out_shape=[
            pltpu.VMEM((KVH - 1, rows, GROUP * HD), jnp.bfloat16),
            pltpu.VMEM((KVH, WINDOW, HD), jnp.bfloat16),
            pltpu.VMEM((2, GROUP * BLK, REACH), jnp.bfloat16),
        ],
        in_specs=[pl.BlockSpec(memory_space=pltpu.HBM)] * 4,
        out_specs=[pl.BlockSpec(memory_space=pltpu.VMEM)] * 3,
        scratch_shapes=[
            pltpu.VMEM((KVH, rows, GROUP * HD), jnp.bfloat16),
            pltpu.VMEM((KVH, WINDOW, HD), jnp.bfloat16),
            pltpu.VMEM((2, REACH, BLK), jnp.bfloat16),
            pltpu.SMEM(doc_flags.shape, jnp.int32),
            pltpu.VMEM((8, BLK), jnp.int32),
            pltpu.VMEM((2, 8, BLK), jnp.int32),
            dma((KVH,)),
            dma((KVH, 2)),
            dma,
            dma((KVH, 3, 2)),
            dma((KVH, 3, 2)),
            dma((KVH, 2, 2)),
            dma((2,)),
            dma((2,)),
        ],
        compiler_params=pltpu.CompilerParams(
            collective_id=0, has_side_effects=True, vmem_limit_bytes=32 * 1024 * 1024
        ),
        name="window_attention",
    )(*inputs)
    return pl.pallas_call(
        last_kernel,
        out_shape=jax.ShapeDtypeStruct(queries.shape, jnp.bfloat16),
        in_specs=[pl.BlockSpec(memory_space=pltpu.VMEM)] * 3,
        out_specs=pl.BlockSpec(memory_space=pltpu.HBM),
        scratch_shapes=[pltpu.VMEM((rows, GROUP * HD), jnp.bfloat16), dma((KVH + 1,))],
        compiler_params=pltpu.CompilerParams(vmem_limit_bytes=32 * 1024 * 1024),
        name="last_group",
    )(*staged)


def solution(mesh):
    spread = P(("groups", "ctx"), None)
    return jax.shard_map(
        functools.partial(per_device, mesh.shape["ctx"]),
        mesh=mesh,
        in_specs=(spread, spread, spread, P(("groups", "ctx"))),
        out_specs=spread,
        check_vma=False,
    )
```

```python
import functools
import math

import jax
import jax.numpy as jnp
from jax import lax
from jax.experimental import pallas as pl
from jax.experimental.pallas import tpu as pltpu
from jax.sharding import PartitionSpec as P

HD = 128
KVH = 4
GROUP = 8
BLK = 128
BACK = 5
NEG_FILL = -1e30
SCALE2 = math.log2(math.e) / math.sqrt(HD)
MESH = pl.DeviceIdType.MESH
SEND_ORDER = (1, 2, 3)

ROWS = {3: (0, BLK), 2: (BLK, 2 * BLK), 1: (3 * BLK, 2 * BLK), 0: (5 * BLK, 2 * BLK)}
WINDOW = 7 * BLK
REACH = 6 * BLK


HEADS = [pl.ds(j * HD, HD) for j in range(GROUP)]


def weigh(i, q_ref, k_ref, bias):
    rows, keys = pl.ds(i * BLK, BLK), pl.ds(i * BLK, REACH)
    key_at = lax.broadcasted_iota(jnp.int32, (BLK, BLK), 0)
    row_at = lax.broadcasted_iota(jnp.int32, (BLK, BLK), 1)
    eye = (key_at == row_at).astype(jnp.bfloat16)
    q = jnp.concatenate(
        [jnp.concatenate([q_ref[rows, head], eye], axis=1) for head in HEADS], axis=0
    )
    k = jnp.concatenate([k_ref[keys, :], bias[i]], axis=1)
    s = lax.dot_general(q, k, (((1,), (1,)), ((), ())), preferred_element_type=jnp.float32)
    top = jnp.max(s, axis=1, keepdims=True) * SCALE2
    return jnp.exp2(s * SCALE2 - top).astype(jnp.bfloat16)


def mix(i, w, v_ref, o_ref):
    rows, keys = pl.ds(i * BLK, BLK), pl.ds(i * BLK, REACH)
    v = jnp.concatenate([v_ref[keys, :], jnp.ones((REACH, HD), jnp.bfloat16)], axis=1)
    mixed = jnp.dot(w, v, preferred_element_type=jnp.float32)
    out = (mixed[:, :HD] / mixed[:, HD:]).astype(jnp.bfloat16)
    for j, head in enumerate(HEADS):
        o_ref[rows, head] = out[j * BLK:(j + 1) * BLK]


def last_kernel(o_first, v_win, w_last, o_hbm, o_buf, sem):
    width, last = GROUP * HD, KVH - 1
    moves = []
    for g in range(last):
        move = pltpu.make_async_copy(
            o_first.at[g], o_hbm.at[:, pl.ds(g * width, width)], sem.at[g]
        )
        move.start()
        moves.append(move)
    for i in range(2):
        mix(i, w_last[i], v_win.at[last], o_buf)
        rows = pl.ds(i * BLK, BLK)
        move = pltpu.make_async_copy(
            o_buf.at[rows, :], o_hbm.at[rows, pl.ds(last * width, width)], sem.at[last + i]
        )
        move.start()
        moves.append(move)
    for move in moves:
        move.wait()


def kernel(
    n, q_hbm, k_hbm, v_hbm, flags_hbm,
    o_buf, v_win, w_last,
    q_buf, k_win, bias, flags_ref, flags_out, flags_in,
    q_sem, own_sem, flag_sem, send_sem, recv_sem, fwd_sem, fsend_sem, frecv_sem,
):
    me = lax.axis_index("ctx")
    core = lax.rem(me, 2)
    even, odd = core == 0, core == 1

    def window(win, g, back):
        start, size = ROWS[back]
        return win.at[g, pl.ds(start, size), :]

    def columns(g):
        return pl.ds(pl.multiple_of(g * HD, HD), HD)

    def q_copy(g):
        cols = pl.ds(pl.multiple_of(g * GROUP * HD, GROUP * HD), GROUP * HD)
        return pltpu.make_async_copy(q_hbm.at[:, cols], q_buf.at[g], q_sem.at[g])

    def own_copies(g):
        return [
            pltpu.make_async_copy(src.at[:, columns(g)], window(win, g, 0), own_sem.at[g, kv])
            for kv, (src, win) in enumerate(((k_hbm, k_win), (v_hbm, v_win)))
        ]

    def sends(g, back):
        size = ROWS[back][1]
        return [
            pltpu.make_async_remote_copy(
                src_ref=win.at[g, pl.ds(WINDOW - size, size), :],
                dst_ref=window(win, g, back),
                send_sem=send_sem.at[g, back - 1, kv],
                recv_sem=recv_sem.at[g, back - 1, kv],
                device_id={"ctx": me + back},
                device_id_type=MESH,
            )
            for kv, win in enumerate((k_win, v_win))
        ]

    def forwards(g, back):
        start, whole = ROWS[back]
        size = ROWS[back + 1][1]
        return [
            pltpu.make_async_remote_copy(
                src_ref=win.at[g, pl.ds(start + whole - size, size), :],
                dst_ref=window(win, g, back + 1),
                send_sem=fwd_sem.at[g, back - 1, kv],
                recv_sem=recv_sem.at[g, back, kv],
                device_id={"ctx": me + 1},
                device_id_type=MESH,
            )
            for kv, win in enumerate((k_win, v_win))
        ]

    def flag_send(back):
        return pltpu.make_async_remote_copy(
            src_ref=flags_out,
            dst_ref=flags_in.at[back - 1],
            send_sem=fsend_sem.at[back - 1],
            recv_sem=frecv_sem.at[back - 1],
            device_id={"ctx": me + back},
            device_id_type=MESH,
        )

    can_send = {
        1: me + 1 < n,
        2: even & (me + 2 < n),
        3: odd & (me + 3 < n),
    }
    direct = {1: me >= 1, 2: even & (me >= 2), 3: even & (me >= 3)}
    present = {back: me >= back for back in (1, 2, 3)}

    flag_copy = pltpu.make_async_copy(flags_hbm, flags_ref, flag_sem)
    flag_copy.start()
    barrier = pltpu.get_barrier_semaphore()
    greet = [
        (1, me + 1 < n), (2, me + 2 < n), (3, can_send[3]),
        (-1, me >= 1), (-2, me >= 2), (-3, direct[3]),
    ]
    for step, there in greet:
        @pl.when(there)
        def _():
            pl.semaphore_signal(barrier, inc=1, device_id={"ctx": me + step}, device_id_type=MESH)

    for g in range(KVH):
        for copy in own_copies(g):
            copy.start()
    flag_copy.wait()
    flags_out[0:1, :] = jnp.full((1, BLK), flags_ref[0], jnp.int32)
    flags_out[1:2, :] = jnp.full((1, BLK), flags_ref[1], jnp.int32)
    flags_out[2:8, :] = jnp.zeros((6, BLK), jnp.int32)

    for back in (1, 2, 3):
        @pl.when(jnp.logical_not(present[back]))
        def _():
            start, size = ROWS[back]
            for win in (k_win, v_win):
                win[:, start:start + size, :] = jnp.zeros((KVH, size, HD), jnp.bfloat16)
            if back < 3:
                flags_in[back - 1] = jnp.zeros((8, BLK), jnp.int32)

    peers = jnp.int32(0)
    for _, there in greet:
        peers = peers + jnp.where(there, 1, 0)
    pl.semaphore_wait(barrier, peers)

    for back in (1, 2):
        @pl.when(me + back < n)
        def _():
            flag_send(back).start()
    batches = [(g, (0, 1)) for g in range(KVH - 1)] + [(KVH - 1, (0,)), (KVH - 1, (1,))]
    for g, kinds in batches:
        for kv in kinds:
            own_copies(g)[kv].wait()
        for back in SEND_ORDER:
            @pl.when(can_send[back])
            def _():
                for kv in kinds:
                    sends(g, back)[kv].start()
        if 0 in kinds:
            q_copy(g).start()

    for back in (1, 2):
        @pl.when(present[back])
        def _():
            flag_send(back).wait_recv()

    mine = flags_out[...]
    begins = {0: mine[0:1], 1: mine[1:2]}
    for back in (1, 2):
        got = flags_in[back - 1]
        begins[-2 * back], begins[1 - 2 * back] = got[0:1], got[1:2]
    key_at = lax.broadcasted_iota(jnp.int32, (BLK, BLK), 0)
    row_at = lax.broadcasted_iota(jnp.int32, (BLK, BLK), 1)
    causal = jnp.where(key_at <= row_at, 0.0, NEG_FILL).astype(jnp.bfloat16)
    for i in range(2):
        bias[i, BACK * BLK:(BACK + 1) * BLK, :] = causal
        hidden = jnp.zeros((1, BLK), jnp.float32)
        for b in range(i - 1, i - BACK - 1, -1):
            hidden = jnp.where(begins[b + 1] != 0, NEG_FILL, hidden)
            at = (b - i + BACK) * BLK
            bias[i, at:at + BLK, :] = jnp.broadcast_to(hidden, (BLK, BLK)).astype(jnp.bfloat16)
    def arrive(g, kinds=(0, 1)):
        def pick(copies):
            return [copies[kv] for kv in kinds]

        for back in (1, 2, 3):
            @pl.when(direct[back])
            def _():
                for copy in pick(sends(g, back)):
                    copy.wait_recv()
            if back < 3:
                @pl.when(even & present[back])
                def _():
                    for copy in pick(forwards(g, back)):
                        copy.start()
        for back in (2, 3):
            @pl.when(odd & present[back])
            def _():
                for copy in pick(forwards(g, back - 1)):
                    copy.wait_recv()
        if 0 in kinds:
            q_copy(g).wait()

    def one_group(g, carry):
        arrive(g)
        for i in range(2):
            mix(i, weigh(i, q_buf.at[g], k_win.at[g], bias), v_win.at[g], o_buf.at[g])
        return carry

    lax.fori_loop(0, KVH - 1, one_group, 0)
    arrive(KVH - 1, (0,))
    for i in range(2):
        w_last[i] = weigh(i, q_buf.at[KVH - 1], k_win.at[KVH - 1], bias)
    arrive(KVH - 1, (1,))

    for back in (1, 2):
        @pl.when(me + back < n)
        def _():
            flag_send(back).wait_send()
    for g in range(KVH):
        for back in (1, 2, 3):
            @pl.when(can_send[back])
            def _():
                for copy in sends(g, back):
                    copy.wait_send()
            if back < 3:
                @pl.when(even & present[back])
                def _():
                    for copy in forwards(g, back):
                        copy.wait_send()


def per_device(n, queries, keys, values, doc_flags):
    rows = queries.shape[0]
    dma = pltpu.SemaphoreType.DMA
    inputs = [
        pltpu.with_memory_space_constraint(x, pltpu.HBM)
        for x in (queries, keys, values, doc_flags)
    ]
    staged = pl.pallas_call(
        functools.partial(kernel, n),
        out_shape=[
            pltpu.VMEM((KVH - 1, rows, GROUP * HD), jnp.bfloat16),
            pltpu.VMEM((KVH, WINDOW, HD), jnp.bfloat16),
            pltpu.VMEM((2, GROUP * BLK, REACH), jnp.bfloat16),
        ],
        in_specs=[pl.BlockSpec(memory_space=pltpu.HBM)] * 4,
        out_specs=[pl.BlockSpec(memory_space=pltpu.VMEM)] * 3,
        scratch_shapes=[
            pltpu.VMEM((KVH, rows, GROUP * HD), jnp.bfloat16),
            pltpu.VMEM((KVH, WINDOW, HD), jnp.bfloat16),
            pltpu.VMEM((2, REACH, BLK), jnp.bfloat16),
            pltpu.SMEM(doc_flags.shape, jnp.int32),
            pltpu.VMEM((8, BLK), jnp.int32),
            pltpu.VMEM((2, 8, BLK), jnp.int32),
            dma((KVH,)),
            dma((KVH, 2)),
            dma,
            dma((KVH, 3, 2)),
            dma((KVH, 3, 2)),
            dma((KVH, 2, 2)),
            dma((2,)),
            dma((2,)),
        ],
        compiler_params=pltpu.CompilerParams(
            collective_id=0, has_side_effects=True, vmem_limit_bytes=32 * 1024 * 1024
        ),
        name="window_attention",
    )(*inputs)
    return pl.pallas_call(
        last_kernel,
        out_shape=jax.ShapeDtypeStruct(queries.shape, jnp.bfloat16),
        in_specs=[pl.BlockSpec(memory_space=pltpu.VMEM)] * 3,
        out_specs=pl.BlockSpec(memory_space=pltpu.HBM),
        scratch_shapes=[pltpu.VMEM((rows, GROUP * HD), jnp.bfloat16), dma((KVH + 1,))],
        compiler_params=pltpu.CompilerParams(vmem_limit_bytes=32 * 1024 * 1024),
        name="last_group",
    )(*staged)


def solution(mesh):
    spread = P(("groups", "ctx"), None)
    return jax.shard_map(
        functools.partial(per_device, mesh.shape["ctx"]),
        mesh=mesh,
        in_specs=(spread, spread, spread, P(("groups", "ctx"))),
        out_specs=spread,
        check_vma=False,
    )
```
